32 devices in a mesh: lat: 4 (over z), lon: 8 (over y, x, core).
Axes of the slice: x: 2, y: 2, z: 4, core: 2. Of those that a mesh axis runs over, the one named last changes fastest.
Arguments:
- fields: float32 [5, 960, 2880], P(None, 'lat', 'lon'), may hold values from -6 to 6
- east_courant: float32 [960, 2880], P('lat', 'lon'), may hold values from -0.4 to 0.4
- north_courant: float32 [960, 2880], P('lat', 'lon'), may hold values from -0.4 to 0.4
- cutoff: int32 [960], replicated, may hold values from 1 to 1439
- damping: float32 [960], replicated, may hold values from 0.05 to 0.5
- ship_rows: int32 [4, 4, 60], replicated, may hold values from -1 to 239, as said below
Outputs:
- updated: float32 [5, 960, 2880], P(None, 'lat', 'lon')
The draws below stay inside these ranges and needn't reach their ends.
Inputs may be any that keep to these rules, and one draw needn't show every extreme that they name: ship_rows[s, d, j] is a row of band s (0 to 239) whose filter is computed by band d, or -1 for an empty slot; no row is listed twice; every row within 240 rows of either pole is listed, no row farther than 360 from both poles is listed, and rows between are listed or not, so that bands 0 and 3 are covered whole; a band's listed rows fill the slots of its destinations in full except the last destination it uses, so band 0 fills 60 slots to some band.
All inputs are finite; a program needn't handle non-finite values.
Results may differ from the reference program's by a relative error of at most 0.0003.
Values sent between devices are 32-bit elements; how exact they have to be, the bound alone decides.
A program may use at most 256 MiB of HBM per device.

```python
import math
import jax
import jax.numpy as jnp

CHANNELS = 5
NLON = 2880
ROWS_DEV = 240
BANDS = 4
NLAT = 960
CAP = 60


def draw_ship_rows(key, part):
    key = jax.random.fold_in(key, 7919)
    key_zone, key_order, key_dest = jax.random.split(key, 3)
    lat_count = ROWS_DEV * BANDS
    lower_bound = ROWS_DEV
    upper_bound = max(lat_count // 4, ROWS_DEV + ROWS_DEV // 2)
    global_rows = jnp.arange(BANDS, dtype=jnp.int32)[:, None] * ROWS_DEV + jnp.arange(ROWS_DEV, dtype=jnp.int32)[None, :]
    pole_distance = jnp.minimum(global_rows, lat_count - 1 - global_rows)
    coin = jax.random.randint(key_zone, (BANDS, ROWS_DEV), 0, 2).astype(jnp.int32)
    listed = jnp.where(pole_distance < lower_bound, 1, jnp.where(pole_distance < upper_bound, coin, 0)).astype(jnp.int32)
    scores = jax.vmap(lambda subkey: jax.random.permutation(subkey, ROWS_DEV))(jax.random.split(key_order, BANDS)).astype(jnp.int32)
    sort_keys = (1 - listed) * ROWS_DEV + scores
    ordering = jnp.argsort(sort_keys, axis=1, stable=True).astype(jnp.int32)
    listed_count = jnp.sum(listed, axis=1)
    destinations = jax.vmap(lambda subkey: jax.random.permutation(subkey, BANDS))(jax.random.split(key_dest, BANDS)).astype(jnp.int32)
    positions = jnp.arange(ROWS_DEV, dtype=jnp.int32)
    target_band = destinations[:, positions // CAP]
    target_slot = jnp.broadcast_to(positions % CAP, (BANDS, ROWS_DEV))
    entries = jnp.where(positions[None, :] < listed_count[:, None], ordering, -1).astype(jnp.int32)
    source_band = jnp.broadcast_to(jnp.arange(BANDS, dtype=jnp.int32)[:, None], (BANDS, ROWS_DEV))
    empty_lists = jnp.full((BANDS, BANDS, CAP), -1, jnp.int32)
    return empty_lists.at[source_band, target_band, target_slot].set(entries)


def place_ends(drawn, rng, low, top_value):
    extent = drawn.shape
    index_at = [jax.random.randint(jax.random.fold_in(rng, axis), (), 0, extent[axis]) for axis in range(len(extent))]
    drawn = drawn.at[tuple(index_at)].set(low)
    longest = extent.index(max(extent))
    index_at[longest] = (index_at[longest] + 1) % extent[longest]
    return drawn.at[tuple(index_at)].set(top_value)


def levels(stream_key, dims, pieces, low, largest):
    def one(axis_at, parts):
        draws = jax.random.uniform(jax.random.fold_in(jax.random.fold_in(stream_key, 6), axis_at), (parts,), jnp.float32, low / len(pieces), largest / len(pieces))
        return jnp.repeat(jnp.exp(draws), dims[axis_at] // parts).reshape((-1,) + (1,) * (len(dims) - axis_at - 1))

    factor_of = one(*pieces[0])
    for cut in pieces[1:]:
        factor_of = factor_of * one(*cut)
    return factor_of


def gaussian(own_key, extent, deviation, limit, cuts=(), kind=jnp.bfloat16):
    array = deviation * jax.random.normal(own_key, extent, jnp.float32)
    if cuts:
        array = array * levels(own_key, extent, cuts, -0.22, 0.18)
    return jnp.clip(array, -limit, limit).astype(kind)


def setup_inputs(seed: int = 0) -> dict:
    keys = jax.random.split(jax.random.key(seed), 7)
    return {
        "fields": gaussian(keys[0], (CHANNELS, NLAT, NLON), 1.0, 6.0, ((1, 4), (2, 8)), jnp.float32),
        "east_courant": jnp.clip(jax.random.uniform(keys[1], (NLAT, NLON), jnp.float32, -0.4, 0.4) * levels(keys[1], (NLAT, NLON), ((0, 4), (1, 8)), -0.4, 0.0), -0.4, 0.4),
        "north_courant": jnp.clip(jax.random.uniform(keys[2], (NLAT, NLON), jnp.float32, -0.4, 0.4) * levels(keys[2], (NLAT, NLON), ((0, 4), (1, 8)), -0.4, 0.0), -0.4, 0.4),
        "cutoff": place_ends(jax.random.randint(keys[3], (NLAT,), 1, NLON // 2), jax.random.fold_in(keys[3], 1), 1, (NLON // 2) - 1).astype(jnp.int32),
        "damping": jnp.clip(jnp.exp(jax.random.uniform(keys[4], (NLAT,), jnp.float32, math.log(0.05), math.log(0.5))), 0.05, 0.5),
        "ship_rows": draw_ship_rows(jax.random.fold_in(keys[6], 71), 0),
    }


def reference(fields, east_courant, north_courant, cutoff, damping, ship_rows):
    lat_count = fields.shape[1]
    lon_count = fields.shape[2]
    east_cells = jnp.roll(fields, -1, axis=2)
    west_cells = jnp.roll(fields, 1, axis=2)
    west_courant = jnp.roll(east_courant, 1, axis=1)
    east_flux = east_courant * jnp.where(east_courant > 0, fields, east_cells)
    west_flux = west_courant * jnp.where(west_courant > 0, west_cells, fields)
    zero_row = jnp.zeros_like(fields[:, :1, :])
    north_cells = jnp.concatenate([fields[:, 1:, :], zero_row], axis=1)
    south_cells = jnp.concatenate([zero_row, fields[:, :-1, :]], axis=1)
    south_courant = jnp.concatenate([jnp.zeros_like(north_courant[:1]), north_courant[:-1]], axis=0)
    global_rows = jnp.arange(lat_count, dtype=jnp.int32)
    latitudes = global_rows.astype(jnp.float32)
    face_n = jnp.sin((latitudes + 1.0) * (math.pi / lat_count))
    face_s = jnp.sin(latitudes * (math.pi / lat_count))
    centre = jnp.sin((latitudes + 0.5) * (math.pi / lat_count))
    north_mask = (global_rows < lat_count - 1).astype(jnp.float32)
    south_mask = (global_rows > 0).astype(jnp.float32)
    north_flux = north_courant * jnp.where(north_courant > 0, fields, north_cells) * (face_n * north_mask)[:, None]
    south_flux = south_courant * jnp.where(south_courant > 0, south_cells, fields) * (face_s * south_mask)[:, None]
    advected = fields - (east_flux - west_flux) - (north_flux - south_flux) / centre[:, None]

    sources = jnp.arange(BANDS, dtype=jnp.int32)[:, None, None]
    listed_rows = sources * ROWS_DEV + ship_rows
    placement = jnp.where(ship_rows >= 0, listed_rows, NLAT).reshape(-1).astype(jnp.int32)
    marked = jnp.zeros((NLAT,), jnp.int32).at[placement].set(1, mode="drop")

    spectrum = jnp.fft.rfft(advected, axis=2)
    wavenumbers = jnp.arange(lon_count // 2 + 1, dtype=jnp.int32)
    response = jnp.where(wavenumbers[None, :] <= cutoff[:, None], jnp.ones_like(damping)[:, None], damping[:, None])
    filtered = jnp.fft.irfft(spectrum * response[None, :, :], n=lon_count, axis=2).astype(jnp.float32)
    return jnp.where(marked[None, :, None] > 0, filtered, advected)
```

```python
import functools
import math

import jax
import jax.numpy as jnp
import numpy as np
from jax import lax
from jax.experimental import pallas as pl
from jax.experimental.pallas import tpu as pltpu
from jax.sharding import PartitionSpec as P

MESH = pl.DeviceIdType.MESH
BF16 = jnp.bfloat16


def ceil_to(value, unit):
    return -(-value // unit) * unit


def chunk_rows(total, pieces):
    tiles = total // 8
    pieces = min(pieces, tiles)
    sizes = [8 * (tiles // pieces + (1 if i < tiles % pieces else 0)) for i in range(pieces)]
    return [(sum(sizes[:i]), sizes[i]) for i in range(pieces)]


def tables(segments, length, width):
    index = np.arange(length, dtype=np.int64)
    angle = (index[:, None] * index[None, :] % length) * (2 * math.pi / length)
    matrix = np.zeros((width, 2 * width), np.float64)
    matrix[:length, :length] = np.cos(angle)
    matrix[:length, width : width + length] = np.sin(angle)
    hi = matrix.astype(np.float32).astype(BF16)
    lo = (matrix - hi.astype(np.float64)).astype(np.float32).astype(BF16)
    stacked = np.concatenate([hi, hi, lo], axis=0)
    half = segments // 2
    twiddle = np.zeros((2 * (half + 1), width), np.float64)
    for residue in range(half + 1):
        turn = (residue * index % (segments * length)) * (2 * math.pi / (segments * length))
        twiddle[2 * residue, :length] = np.cos(turn)
        twiddle[2 * residue + 1, :length] = np.sin(turn)
    return stacked, twiddle.astype(np.float32)


def real_dft(parts):
    count = len(parts)
    if count == 1:
        return [(parts[0], None)]
    if count == 2:
        return [(parts[0] + parts[1], None), (parts[0] - parts[1], None)]
    half, quarter = count // 2, count // 4
    even, odd = real_dft(parts[0::2]), real_dft(parts[1::2])
    spectrum = [None] * (half + 1)
    for k in range(quarter + 1):
        er, ei = even[k]
        orr, oi = odd[k]
        if k == 0:
            spectrum[0] = (er + orr, None)
            spectrum[half] = (er - orr, None)
        elif k == quarter:
            spectrum[k] = (er, -orr)
        else:
            c, s = math.cos(2 * math.pi * k / count), math.sin(2 * math.pi * k / count)
            tr = c * orr + s * oi
            ti = c * oi - s * orr
            spectrum[k] = (er + tr, ei + ti)
            spectrum[half - k] = (er - tr, ti - ei)
    return spectrum


def real_idft(spectrum):
    half = len(spectrum) - 1
    count = 2 * half
    if count == 2:
        a, b = spectrum[0][0], spectrum[1][0]
        return [a + b, a - b]
    quarter = half // 2
    even, odd = [None] * (quarter + 1), [None] * (quarter + 1)
    for k in range(quarter + 1):
        if k == 0:
            a, b = spectrum[0][0], spectrum[half][0]
            even[0], odd[0] = (a + b, None), (a - b, None)
        elif k == quarter:
            a, b = spectrum[k]
            even[k], odd[k] = (2.0 * a, None), (-2.0 * b, None)
        else:
            ar, ai = spectrum[k]
            br, bi = spectrum[half - k]
            even[k] = (ar + br, ai - bi)
            dr, di = ar - br, ai + bi
            c, s = math.cos(2 * math.pi * k / count), math.sin(2 * math.pi * k / count)
            odd[k] = (c * dr - s * di, s * dr + c * di)
    out = [None] * count
    out[0::2] = real_idft(even)
    out[1::2] = real_idft(odd)
    return out


def filter_rows(parts, cut, damp, weight, twiddle, spread, length):
    segments = len(parts)
    half = segments // 2
    rows, width = parts[0].shape
    total = segments * length
    stride = ceil_to(rows, 16)
    slots = 0

    def put(value):
        nonlocal slots
        hi = value.astype(BF16)
        lo = (value - hi.astype(jnp.float32)).astype(BF16)
        here = pl.ds(slots * stride, rows)
        spread[here, 0:width] = hi
        spread[here, width : 2 * width] = lo
        spread[here, 2 * width : 3 * width] = hi
        slots += 1
        return slots - 1

    def multiply():
        return jnp.dot(
            spread[0 : slots * stride, :], weight[...], preferred_element_type=jnp.float32
        )

    def pick(product, slot, which):
        return product[slot * stride : slot * stride + rows, which * width : (which + 1) * width]

    places = []
    for k, (re, im) in enumerate(real_dft(parts)):
        if k == 0:
            places.append((put(re), None))
            continue
        c, s = twiddle[2 * k : 2 * k + 1, :], twiddle[2 * k + 1 : 2 * k + 2, :]
        if im is None:
            places.append((put(re * c), put(-(re * s))))
        else:
            places.append((put(re * c + im * s), put(im * c - re * s)))
    product = multiply()
    slots = 0
    scale = 1.0 / total
    pass_band = jnp.float32(scale)
    stop_band = damp * jnp.float32(scale)
    lane = lax.broadcasted_iota(jnp.int32, (rows, width), 1)
    back = []
    for k, (a, b) in enumerate(places):
        wave = k + segments * lane
        response = jnp.where(jnp.minimum(wave, total - wave) <= cut, pass_band, stop_band)
        re, im = pick(product, a, 0), -pick(product, a, 1)
        if b is not None:
            re, im = re + pick(product, b, 1), im + pick(product, b, 0)
        back.append((put(re * response), put(im * response)))
    product = multiply()
    spectrum = []
    for k, (a, b) in enumerate(back):
        re = pick(product, a, 0) - pick(product, b, 1)
        if k == 0:
            spectrum.append((re, None))
            continue
        im = pick(product, b, 0) + pick(product, a, 1)
        c, s = twiddle[2 * k : 2 * k + 1, :], twiddle[2 * k + 1 : 2 * k + 2, :]
        if k == half:
            spectrum.append((re * c - im * s, None))
        else:
            spectrum.append((re * c - im * s, im * c + re * s))
    return real_idft(spectrum)


def filter_kernel(
    segments, length, chunks,
    advected, cut_ref, damp_ref, weight, twiddle, out_ref,
    gathered, results, spread, send_a, recv_a, send_b, recv_b,
):
    me = lax.axis_index("lon")
    peers = [lax.rem(me + p, segments) for p in range(1, segments)]
    barrier = pltpu.get_barrier_semaphore()
    for peer in peers:
        pl.semaphore_signal(barrier, inc=1, device_id={"lon": peer}, device_id_type=MESH)
    pl.semaphore_wait(barrier, segments - 1)
    outward, homeward = [], []
    for c, (start, rows) in enumerate(chunks):
        window = pl.ds(start, rows)
        for p, peer in enumerate(peers):
            copy = pltpu.make_async_remote_copy(
                src_ref=advected.at[peer, window],
                dst_ref=gathered.at[me, window],
                send_sem=send_a.at[c, p],
                recv_sem=recv_a.at[c, p],
                device_id={"lon": peer},
                device_id_type=MESH,
            )
            copy.start()
            outward.append(copy)
    for c, (start, rows) in enumerate(chunks):
        window = pl.ds(start, rows)
        gathered[me, window] = advected[me, window]
        for p in range(segments - 1):
            outward[c * (segments - 1) + p].wait_recv()
        filtered = filter_rows(
            [gathered[j, window] for j in range(segments)],
            cut_ref[window, :], damp_ref[window, :], weight, twiddle, spread, length,
        )
        for j in range(segments):
            results[j, window] = filtered[j]
        for p, peer in enumerate(peers):
            copy = pltpu.make_async_remote_copy(
                src_ref=results.at[peer, window],
                dst_ref=out_ref.at[me, window],
                send_sem=send_b.at[c, p],
                recv_sem=recv_b.at[c, p],
                device_id={"lon": peer},
                device_id_type=MESH,
            )
            copy.start()
            homeward.append(copy)
        out_ref[me, window] = results[me, window]
    for copy in outward:
        copy.wait_send()
    for copy in homeward:
        copy.wait()


def circle_filter(advected, cut_rows, damp_rows, pieces=3):
    segments = lax.axis_size("lon")
    channels, rows_dev, length = advected.shape
    width = ceil_to(length, 128)
    share = ceil_to(ceil_to(channels * rows_dev, segments) // segments, 8)
    padded = share * segments
    chunks = chunk_rows(share, pieces)
    weight, twiddle = tables(segments, length, width)
    slots = segments + 2
    flat = jnp.pad(
        advected.reshape(channels * rows_dev, length),
        ((0, padded - channels * rows_dev), (0, width - length)),
    ).reshape(segments, share, width)
    me = lax.axis_index("lon")

    def mine(values):
        column = jnp.pad(jnp.tile(values, channels), (0, padded - channels * rows_dev))
        return lax.dynamic_slice_in_dim(column, me * share, share)[:, None]

    depth = slots * ceil_to(max(rows for _, rows in chunks), 16)
    semaphores = pltpu.SemaphoreType.DMA((len(chunks), segments - 1))
    filtered = pl.pallas_call(
        functools.partial(filter_kernel, segments, length, chunks),
        out_shape=jax.ShapeDtypeStruct((segments, share, width), jnp.float32),
        in_specs=[pl.BlockSpec(memory_space=pltpu.VMEM)] * 5,
        out_specs=pl.BlockSpec(memory_space=pltpu.VMEM),
        scratch_shapes=[
            pltpu.VMEM((segments, share, width), jnp.float32),
            pltpu.VMEM((segments, share, width), jnp.float32),
            pltpu.VMEM((depth, 3 * width), BF16),
            semaphores, semaphores, semaphores, semaphores,
        ],
        compiler_params=pltpu.CompilerParams(
            collective_id=0, has_side_effects=True, vmem_limit_bytes=56 * 1024 * 1024
        ),
    )(flat, mine(cut_rows), mine(damp_rows), jnp.asarray(weight), jnp.asarray(twiddle))
    return filtered.reshape(padded, width)[: channels * rows_dev, :length].reshape(advected.shape)


def shifted(cells, axis, step, closed):
    count = lax.axis_size(axis)
    pairs = [(i, (i + step) % count) for i in range(count) if closed or 0 <= i + step < count]
    return lax.ppermute(cells, axis, pairs)


def per_device(fields, east_courant, north_courant, cutoff, damping, ship_rows):
    channels, rows_dev, length = fields.shape
    bands = lax.axis_size("lat")
    lat_count = rows_dev * bands
    band = lax.axis_index("lat")
    stacked_east = jnp.concatenate([fields[:, :, -1], east_courant[None, :, -1]], axis=0)
    west_edge = shifted(stacked_east, "lon", 1, True)
    east_edge = shifted(fields[:, :, 0], "lon", -1, True)
    stacked_north = jnp.concatenate([fields[:, -1, :], north_courant[None, -1, :]], axis=0)
    south_edge = shifted(stacked_north, "lat", 1, False)
    north_edge = shifted(fields[:, 0, :], "lat", -1, False)
    east_cells = jnp.concatenate([fields[:, :, 1:], east_edge[:, :, None]], axis=2)
    west_cells = jnp.concatenate([west_edge[:channels, :, None], fields[:, :, :-1]], axis=2)
    west_courant = jnp.concatenate([west_edge[channels, :, None], east_courant[:, :-1]], axis=1)
    north_cells = jnp.concatenate([fields[:, 1:, :], north_edge[:, None, :]], axis=1)
    south_cells = jnp.concatenate([south_edge[:channels, None, :], fields[:, :-1, :]], axis=1)
    south_courant = jnp.concatenate([south_edge[channels, None, :], north_courant[:-1]], axis=0)
    east_flux = east_courant * jnp.where(east_courant > 0, fields, east_cells)
    west_flux = west_courant * jnp.where(west_courant > 0, west_cells, fields)
    global_rows = band * rows_dev + jnp.arange(rows_dev, dtype=jnp.int32)
    latitudes = global_rows.astype(jnp.float32)
    face_n = jnp.sin((latitudes + 1.0) * (math.pi / lat_count))
    face_s = jnp.sin(latitudes * (math.pi / lat_count))
    centre = jnp.sin((latitudes + 0.5) * (math.pi / lat_count))
    face_n = jnp.where(global_rows < lat_count - 1, face_n, 0.0)
    face_s = jnp.where(global_rows > 0, face_s, 0.0)
    north_flux = north_courant * jnp.where(north_courant > 0, fields, north_cells) * face_n[:, None]
    south_flux = south_courant * jnp.where(south_courant > 0, south_cells, fields) * face_s[:, None]
    advected = fields - (east_flux - west_flux) - (north_flux - south_flux) / centre[:, None]
    cut_rows = lax.dynamic_slice_in_dim(cutoff, band * rows_dev, rows_dev)
    damp_rows = lax.dynamic_slice_in_dim(damping, band * rows_dev, rows_dev)
    listed = lax.dynamic_index_in_dim(ship_rows, band, axis=0, keepdims=False).reshape(-1)
    polar = jnp.any(listed[:, None] == jnp.arange(rows_dev, dtype=jnp.int32)[None, :], axis=0)
    filtered = circle_filter(advected, cut_rows, damp_rows)
    return jnp.where(polar[None, :, None], filtered, advected)


def solution(mesh):
    placed = (P(None, "lat", "lon"), P("lat", "lon"), P("lat", "lon"), P(), P(), P())
    return jax.shard_map(
        per_device, mesh=mesh, in_specs=placed, out_specs=P(None, "lat", "lon"), check_vma=False
    )
```

```python
import functools
import math

import jax
import jax.numpy as jnp
import numpy as np
from jax import lax
from jax.experimental import pallas as pl
from jax.experimental.pallas import tpu as pltpu
from jax.sharding import PartitionSpec as P

MESH = pl.DeviceIdType.MESH
BF16 = jnp.bfloat16


def ceil_to(value, unit):
    return -(-value // unit) * unit


def chunk_rows(total, pieces):
    tiles = total // 8
    pieces = min(pieces, tiles)
    sizes = [8 * (tiles // pieces + (1 if i < tiles % pieces else 0)) for i in range(pieces)]
    return [(sum(sizes[:i]), sizes[i]) for i in range(pieces)]


def tables(segments, length, width):
    index = np.arange(length, dtype=np.int64)
    angle = (index[:, None] * index[None, :] % length) * (2 * math.pi / length)
    matrix = np.zeros((width, 2 * width), np.float64)
    matrix[:length, :length] = np.cos(angle)
    matrix[:length, width : width + length] = np.sin(angle)
    hi = matrix.astype(np.float32).astype(BF16)
    lo = (matrix - hi.astype(np.float64)).astype(np.float32).astype(BF16)
    stacked = np.concatenate([hi, hi, lo], axis=0)
    half = segments // 2
    twiddle = np.zeros((2 * (half + 1), width), np.float64)
    for residue in range(half + 1):
        turn = (residue * index % (segments * length)) * (2 * math.pi / (segments * length))
        twiddle[2 * residue, :length] = np.cos(turn)
        twiddle[2 * residue + 1, :length] = np.sin(turn)
    return stacked, twiddle.astype(np.float32)


def real_dft(parts):
    count = len(parts)
    if count == 1:
        return [(parts[0], None)]
    if count == 2:
        return [(parts[0] + parts[1], None), (parts[0] - parts[1], None)]
    half, quarter = count // 2, count // 4
    even, odd = real_dft(parts[0::2]), real_dft(parts[1::2])
    spectrum = [None] * (half + 1)
    for k in range(quarter + 1):
        er, ei = even[k]
        orr, oi = odd[k]
        if k == 0:
            spectrum[0] = (er + orr, None)
            spectrum[half] = (er - orr, None)
        elif k == quarter:
            spectrum[k] = (er, -orr)
        else:
            c, s = math.cos(2 * math.pi * k / count), math.sin(2 * math.pi * k / count)
            tr = c * orr + s * oi
            ti = c * oi - s * orr
            spectrum[k] = (er + tr, ei + ti)
            spectrum[half - k] = (er - tr, ti - ei)
    return spectrum


def real_idft(spectrum):
    half = len(spectrum) - 1
    count = 2 * half
    if count == 2:
        a, b = spectrum[0][0], spectrum[1][0]
        return [a + b, a - b]
    quarter = half // 2
    even, odd = [None] * (quarter + 1), [None] * (quarter + 1)
    for k in range(quarter + 1):
        if k == 0:
            a, b = spectrum[0][0], spectrum[half][0]
            even[0], odd[0] = (a + b, None), (a - b, None)
        elif k == quarter:
            a, b = spectrum[k]
            even[k], odd[k] = (2.0 * a, None), (-2.0 * b, None)
        else:
            ar, ai = spectrum[k]
            br, bi = spectrum[half - k]
            even[k] = (ar + br, ai - bi)
            dr, di = ar - br, ai + bi
            c, s = math.cos(2 * math.pi * k / count), math.sin(2 * math.pi * k / count)
            odd[k] = (c * dr - s * di, s * dr + c * di)
    out = [None] * count
    out[0::2] = real_idft(even)
    out[1::2] = real_idft(odd)
    return out


def filter_rows(parts, cut, damp, weight, twiddle, spread, length):
    segments = len(parts)
    half = segments // 2
    rows, width = parts[0].shape
    total = segments * length
    stride = ceil_to(rows, 16)
    slots = 0

    def put(value):
        nonlocal slots
        hi = value.astype(BF16)
        lo = (value - hi.astype(jnp.float32)).astype(BF16)
        here = pl.ds(slots * stride, rows)
        spread[here, 0:width] = hi
        spread[here, width : 2 * width] = lo
        spread[here, 2 * width : 3 * width] = hi
        slots += 1
        return slots - 1

    def multiply():
        return jnp.dot(
            spread[0 : slots * stride, :], weight[...], preferred_element_type=jnp.float32
        )

    def pick(product, slot, which):
        return product[slot * stride : slot * stride + rows, which * width : (which + 1) * width]

    places = []
    for k, (re, im) in enumerate(real_dft(parts)):
        if k == 0:
            places.append((put(re), None))
            continue
        c, s = twiddle[2 * k : 2 * k + 1, :], twiddle[2 * k + 1 : 2 * k + 2, :]
        if im is None:
            places.append((put(re * c), put(-(re * s))))
        else:
            places.append((put(re * c + im * s), put(im * c - re * s)))
    product = multiply()
    slots = 0
    scale = 1.0 / total
    pass_band = jnp.float32(scale)
    stop_band = damp * jnp.float32(scale)
    lane = lax.broadcasted_iota(jnp.int32, (rows, width), 1)
    back = []
    for k, (a, b) in enumerate(places):
        wave = k + segments * lane
        response = jnp.where(jnp.minimum(wave, total - wave) <= cut, pass_band, stop_band)
        re, im = pick(product, a, 0), -pick(product, a, 1)
        if b is not None:
            re, im = re + pick(product, b, 1), im + pick(product, b, 0)
        back.append((put(re * response), put(im * response)))
    product = multiply()
    spectrum = []
    for k, (a, b) in enumerate(back):
        re = pick(product, a, 0) - pick(product, b, 1)
        if k == 0:
            spectrum.append((re, None))
            continue
        im = pick(product, b, 0) + pick(product, a, 1)
        c, s = twiddle[2 * k : 2 * k + 1, :], twiddle[2 * k + 1 : 2 * k + 2, :]
        if k == half:
            spectrum.append((re * c - im * s, None))
        else:
            spectrum.append((re * c - im * s, im * c + re * s))
    return real_idft(spectrum)


def spans(start, count, rows_dev, channels):
    pieces, at, end = [], start, min(start + count, channels * rows_dev)
    while at < end:
        channel, row = divmod(at, rows_dev)
        take = min(end - at, rows_dev - row)
        pieces.append((at - start, channel, row, take))
        at += take
    return pieces


def pad_lanes(value, width):
    rows, length = value.shape
    if width == length:
        return value
    return jnp.concatenate([value, jnp.zeros((rows, width - length), value.dtype)], axis=1)


def step_kernel(
    segments, bands, chunks, share,
    fields_hbm, east_hbm, north_hbm, cutoff, damping, ship, weight_hbm, twiddle, out_ref,
    cells, east, north, weight, facts, edge_out, edge_in, advected, gathered, results,
    returned, spread, cut_ref, damp_ref, polar,
    load_sem, halo_send, halo_recv, send_a, recv_a, send_b, recv_b,
):
    channels, rows_dev, length = fields_hbm.shape
    width = advected.shape[2]
    lat_count = rows_dev * bands
    body = pl.ds(8, rows_dev)
    me, band = lax.axis_index("lon"), lax.axis_index("lat")
    right, left = lax.rem(me + 1, segments), lax.rem(me + segments - 1, segments)
    peers = [lax.rem(me + p, segments) for p in range(1, segments)]
    loads = [
        pltpu.make_async_copy(fields_hbm, cells.at[:, body], load_sem.at[0]),
        pltpu.make_async_copy(north_hbm, north.at[body], load_sem.at[1]),
        pltpu.make_async_copy(east_hbm, east, load_sem.at[2]),
        pltpu.make_async_copy(weight_hbm, weight, load_sem.at[3]),
    ]
    for load in loads:
        load.start()
    barrier = pltpu.get_barrier_semaphore()
    for peer in peers:
        pl.semaphore_signal(barrier, inc=1, device_id={"lon": peer}, device_id_type=MESH)

    @pl.when(band > 0)
    def _():
        pl.semaphore_signal(barrier, inc=1, device_id={"lat": band - 1}, device_id_type=MESH)

    @pl.when(band < bands - 1)
    def _():
        pl.semaphore_signal(barrier, inc=1, device_id={"lat": band + 1}, device_id_type=MESH)

    @pl.when(band == 0)
    def _():
        cells[:, 0:8, :] = jnp.zeros((channels, 8, length), jnp.float32)
        north[0:8, :] = jnp.zeros((8, length), jnp.float32)

    @pl.when(band == bands - 1)
    def _():
        cells[:, rows_dev + 8 : rows_dev + 16, :] = jnp.zeros((channels, 8, length), jnp.float32)

    row = band * rows_dev + lax.broadcasted_iota(jnp.int32, (rows_dev, 128), 0)
    lane = lax.broadcasted_iota(jnp.int32, (rows_dev, 128), 1)
    shift = jnp.where(lane == 0, 1.0, jnp.where(lane == 1, 0.0, 0.5))
    facts[...] = jnp.sin((row.astype(jnp.float32) + shift) * (math.pi / lat_count))

    for load in loads[:3]:
        load.wait()
    for c in range(channels):
        edge_out[0, :, c : c + 1] = cells[c, body, length - 1 : length]
        edge_out[1, :, c : c + 1] = cells[c, body, 0:1]
    edge_out[0, :, channels : channels + 1] = east[:, length - 1 : length]
    beside = jnp.where(band > 0, 1, 0) + jnp.where(band < bands - 1, 1, 0)
    pl.semaphore_wait(barrier, segments - 1 + beside)

    def halo(source, target, slot, place):
        return pltpu.make_async_remote_copy(
            src_ref=source, dst_ref=target, send_sem=halo_send.at[slot],
            recv_sem=halo_recv.at[slot], device_id=place, device_id_type=MESH,
        )

    first, last = pl.ds(8, 8), pl.ds(rows_dev, 8)
    above = pl.ds(rows_dev + 8, 8)
    up = {"lat": jnp.minimum(band + 1, bands - 1)}
    down = {"lat": jnp.maximum(band - 1, 0)}
    northward = [
        halo(cells.at[:, last], cells.at[:, pl.ds(0, 8)], 0, up),
        halo(north.at[last], north.at[pl.ds(0, 8)], 1, up),
    ]
    southward = halo(cells.at[:, first], cells.at[:, above], 2, down)
    sideways = [
        halo(edge_out.at[0], edge_in.at[0], 3, {"lon": right}),
        halo(edge_out.at[1], edge_in.at[1], 4, {"lon": left}),
    ]
    for copy in sideways:
        copy.start()

    @pl.when(band < bands - 1)
    def _():
        for copy in northward:
            copy.start()

    @pl.when(band > 0)
    def _():
        southward.start()

    flat = me * share + lax.broadcasted_iota(jnp.int32, (share, lat_count), 0)
    wanted = band * rows_dev + lax.rem(flat, rows_dev)
    hit = wanted == lax.broadcasted_iota(jnp.int32, (share, lat_count), 1)
    cut_ref[...] = jnp.sum(jnp.where(hit, cutoff[...].astype(jnp.float32), 0.0), axis=1, keepdims=True)
    damp_ref[...] = jnp.sum(jnp.where(hit, damping[...], 0.0), axis=1, keepdims=True)
    listed = ship[pl.ds(band, 1), :]
    own = lax.broadcasted_iota(jnp.int32, (rows_dev, listed.shape[1]), 0)
    polar[...] = jnp.sum(jnp.where(own == listed, 1.0, 0.0), axis=1, keepdims=True)
    spread[...] = jnp.zeros_like(spread)
    for j in range(segments):
        filled = min(max(channels * rows_dev - j * share, 0), share)
        if filled < share:
            advected[j, filled:share, :] = jnp.zeros((share - filled, width), jnp.float32)

    for copy in sideways:
        copy.wait()

    @pl.when(band < bands - 1)
    def _():
        for copy in northward:
            copy.wait_send()
        southward.wait_recv()

    @pl.when(band > 0)
    def _():
        southward.wait_send()
        for copy in northward:
            copy.wait_recv()

    def advect(channel, r, rows):
        here = pl.ds(r, rows)
        field = pad_lanes(cells[channel, pl.ds(r + 8, rows), :], width)
        upper = pad_lanes(cells[channel, pl.ds(r + 9, rows), :], width)
        lower = pad_lanes(cells[channel, pl.ds(r + 7, rows), :], width)
        courant_e = pad_lanes(east[here, :], width)
        courant_n = pad_lanes(north[pl.ds(r + 8, rows), :], width)
        courant_s = pad_lanes(north[pl.ds(r + 7, rows), :], width)
        column = lax.broadcasted_iota(jnp.int32, (rows, width), 1)
        grow = band * rows_dev + r + lax.broadcasted_iota(jnp.int32, (rows, 1), 0)
        east_cell = edge_in[1, here, channel : channel + 1]
        west_cell = edge_in[0, here, channel : channel + 1]
        west_courant = edge_in[0, here, channels : channels + 1]
        ahead = jnp.where(column == length - 1, east_cell, pltpu.roll(field, width - 1, 1))
        east_flux = courant_e * jnp.where(courant_e > 0, field, ahead)
        entering = west_courant * jnp.where(west_courant > 0, west_cell, field[:, 0:1])
        west_flux = jnp.where(column == 0, entering, pltpu.roll(east_flux, 1, 1))
        west_flux = jnp.where(column < length, west_flux, 0.0)
        face_n, face_s = facts[here, 0:1], facts[here, 1:2]
        north_flux = courant_n * jnp.where(courant_n > 0, field, upper) * face_n
        south_flux = courant_s * jnp.where(courant_s > 0, lower, field) * face_s
        north_flux = jnp.where(grow < lat_count - 1, north_flux, 0.0)
        south_flux = jnp.where(grow > 0, south_flux, 0.0)
        return field - (east_flux - west_flux) - (north_flux - south_flux) * (1.0 / facts[here, 2:3])

    outward, homeward = [], []
    for c, (start, rows) in enumerate(chunks):
        window = pl.ds(start, rows)
        for j in range(segments):
            for offset, channel, r, count in spans(j * share + start, rows, rows_dev, channels):
                advected[j, start + offset : start + offset + count, :] = advect(channel, r, count)
        for p, peer in enumerate(peers):
            copy = pltpu.make_async_remote_copy(
                src_ref=advected.at[peer, window],
                dst_ref=gathered.at[me, window],
                send_sem=send_a.at[c, p],
                recv_sem=recv_a.at[c, p],
                device_id={"lon": peer},
                device_id_type=MESH,
            )
            copy.start()
            outward.append(copy)
    loads[3].wait()
    for c, (start, rows) in enumerate(chunks):
        window = pl.ds(start, rows)
        gathered[me, window] = advected[me, window]
        for p in range(segments - 1):
            outward[c * (segments - 1) + p].wait_recv()
        filtered = filter_rows(
            [gathered[j, window] for j in range(segments)],
            cut_ref[window, :].astype(jnp.int32), damp_ref[window, :], weight, twiddle, spread,
            length,
        )
        for j in range(segments):
            results[j, window] = filtered[j]
        for p, peer in enumerate(peers):
            copy = pltpu.make_async_remote_copy(
                src_ref=results.at[peer, window],
                dst_ref=returned.at[me, window],
                send_sem=send_b.at[c, p],
                recv_sem=recv_b.at[c, p],
                device_id={"lon": peer},
                device_id_type=MESH,
            )
            copy.start()
            homeward.append(copy)
        returned[me, window] = results[me, window]
    for c, (start, rows) in enumerate(chunks):
        for p in range(segments - 1):
            homeward[c * (segments - 1) + p].wait_recv()
        for j in range(segments):
            for offset, channel, r, count in spans(j * share + start, rows, rows_dev, channels):
                here = slice(start + offset, start + offset + count)
                chosen = jnp.where(polar[r : r + count, :] > 0.0, returned[j, here, :], advected[j, here, :])
                out_ref[channel, r : r + count, :] = chosen[:, :length]
    for copy in outward + homeward:
        copy.wait_send()


def per_device(pieces, fields, east_courant, north_courant, cutoff, damping, ship_rows):
    channels, rows_dev, length = fields.shape
    segments, bands = lax.axis_size("lon"), lax.axis_size("lat")
    width = ceil_to(length, 128)
    share = ceil_to(ceil_to(channels * rows_dev, segments) // segments, 8)
    chunks = chunk_rows(share, pieces)
    weight, twiddle = tables(segments, length, width)
    depth = (segments + 2) * ceil_to(max(rows for _, rows in chunks), 16)
    semaphores = pltpu.SemaphoreType.DMA((len(chunks), segments - 1))
    block = pltpu.VMEM((segments, share, width), jnp.float32)
    whole, local = pl.BlockSpec(memory_space=pl.ANY), pl.BlockSpec(memory_space=pltpu.VMEM)
    return pl.pallas_call(
        functools.partial(step_kernel, segments, bands, chunks, share),
        out_shape=jax.ShapeDtypeStruct(fields.shape, jnp.float32),
        in_specs=[whole, whole, whole, local, local, local, whole, local],
        out_specs=local,
        scratch_shapes=[
            pltpu.VMEM((channels, rows_dev + 16, length), jnp.float32),
            pltpu.VMEM((rows_dev, length), jnp.float32),
            pltpu.VMEM((rows_dev + 16, length), jnp.float32),
            pltpu.VMEM(weight.shape, BF16),
            pltpu.VMEM((rows_dev, 128), jnp.float32),
            pltpu.VMEM((2, rows_dev, 128), jnp.float32),
            pltpu.VMEM((2, rows_dev, 128), jnp.float32),
            block, block, block, block,
            pltpu.VMEM((depth, 3 * width), BF16),
            pltpu.VMEM((share, 1), jnp.float32),
            pltpu.VMEM((share, 1), jnp.float32),
            pltpu.VMEM((rows_dev, 1), jnp.float32),
            pltpu.SemaphoreType.DMA((4,)),
            pltpu.SemaphoreType.DMA((5,)),
            pltpu.SemaphoreType.DMA((5,)),
            semaphores, semaphores, semaphores, semaphores,
        ],
        compiler_params=pltpu.CompilerParams(
            collective_id=0, has_side_effects=True, vmem_limit_bytes=56 * 1024 * 1024
        ),
    )(
        fields, east_courant, north_courant, cutoff[None, :], damping[None, :],
        ship_rows.reshape(bands, -1), jnp.asarray(weight), jnp.asarray(twiddle),
    )


def solution(mesh):
    placed = (P(None, "lat", "lon"), P("lat", "lon"), P("lat", "lon"), P(), P(), P())
    return jax.shard_map(
        functools.partial(per_device, 3), mesh=mesh, in_specs=placed, out_specs=P(None, "lat", "lon"), check_vma=False
    )
```

```python
import functools
import math

import jax
import jax.numpy as jnp
import numpy as np
from jax import lax
from jax.experimental import pallas as pl
from jax.experimental.pallas import tpu as pltpu
from jax.sharding import PartitionSpec as P

MESH = pl.DeviceIdType.MESH
BF16 = jnp.bfloat16


def ceil_to(value, unit):
    return -(-value // unit) * unit


def chunk_rows(total, pieces):
    tiles = total // 8
    pieces = min(pieces, tiles)
    sizes = [8 * (tiles // pieces + (1 if i < tiles % pieces else 0)) for i in range(pieces)]
    return [(sum(sizes[:i]), sizes[i]) for i in range(pieces)]


def tables(segments, length, width):
    index = np.arange(length, dtype=np.int64)
    angle = (index[:, None] * index[None, :] % length) * (2 * math.pi / length)
    matrix = np.zeros((width, 2 * width), np.float64)
    matrix[:length, :length] = np.cos(angle)
    matrix[:length, width : width + length] = np.sin(angle)
    hi = matrix.astype(np.float32).astype(BF16)
    lo = (matrix - hi.astype(np.float64)).astype(np.float32).astype(BF16)
    stacked = np.concatenate([hi, hi, lo], axis=0)
    half = segments // 2
    twiddle = np.zeros((2 * (half + 1), width), np.float64)
    for residue in range(half + 1):
        turn = (residue * index % (segments * length)) * (2 * math.pi / (segments * length))
        twiddle[2 * residue, :length] = np.cos(turn)
        twiddle[2 * residue + 1, :length] = np.sin(turn)
    return stacked, twiddle.astype(np.float32)


def real_dft(parts):
    count = len(parts)
    if count == 1:
        return [(parts[0], None)]
    if count == 2:
        return [(parts[0] + parts[1], None), (parts[0] - parts[1], None)]
    half, quarter = count // 2, count // 4
    even, odd = real_dft(parts[0::2]), real_dft(parts[1::2])
    spectrum = [None] * (half + 1)
    for k in range(quarter + 1):
        er, ei = even[k]
        orr, oi = odd[k]
        if k == 0:
            spectrum[0] = (er + orr, None)
            spectrum[half] = (er - orr, None)
        elif k == quarter:
            spectrum[k] = (er, -orr)
        else:
            c, s = math.cos(2 * math.pi * k / count), math.sin(2 * math.pi * k / count)
            tr = c * orr + s * oi
            ti = c * oi - s * orr
            spectrum[k] = (er + tr, ei + ti)
            spectrum[half - k] = (er - tr, ti - ei)
    return spectrum


def real_idft(spectrum):
    half = len(spectrum) - 1
    count = 2 * half
    if count == 2:
        a, b = spectrum[0][0], spectrum[1][0]
        return [a + b, a - b]
    quarter = half // 2
    even, odd = [None] * (quarter + 1), [None] * (quarter + 1)
    for k in range(quarter + 1):
        if k == 0:
            a, b = spectrum[0][0], spectrum[half][0]
            even[0], odd[0] = (a + b, None), (a - b, None)
        elif k == quarter:
            a, b = spectrum[k]
            even[k], odd[k] = (2.0 * a, None), (-2.0 * b, None)
        else:
            ar, ai = spectrum[k]
            br, bi = spectrum[half - k]
            even[k] = (ar + br, ai - bi)
            dr, di = ar - br, ai + bi
            c, s = math.cos(2 * math.pi * k / count), math.sin(2 * math.pi * k / count)
            odd[k] = (c * dr - s * di, s * dr + c * di)
    out = [None] * count
    out[0::2] = real_idft(even)
    out[1::2] = real_idft(odd)
    return out


def filter_rows(parts, cut, damp, weight, twiddle, spread, length):
    segments = len(parts)
    half = segments // 2
    rows, width = parts[0].shape
    total = segments * length
    stride = ceil_to(rows, 16)
    slots = 0

    def put(value):
        nonlocal slots
        hi = value.astype(BF16)
        lo = (value - hi.astype(jnp.float32)).astype(BF16)
        here = pl.ds(slots * stride, rows)
        spread[here, 0:width] = hi
        spread[here, width : 2 * width] = lo
        spread[here, 2 * width : 3 * width] = hi
        slots += 1
        return slots - 1

    def multiply():
        return jnp.dot(
            spread[0 : slots * stride, :], weight[...], preferred_element_type=jnp.float32
        )

    def pick(product, slot, which):
        return product[slot * stride : slot * stride + rows, which * width : (which + 1) * width]

    places = []
    for k, (re, im) in enumerate(real_dft(parts)):
        if k == 0:
            places.append((put(re), None))
            continue
        c, s = twiddle[2 * k : 2 * k + 1, :], twiddle[2 * k + 1 : 2 * k + 2, :]
        if im is None:
            places.append((put(re * c), put(-(re * s))))
        else:
            places.append((put(re * c + im * s), put(im * c - re * s)))
    product = multiply()
    slots = 0
    scale = 1.0 / total
    pass_band = jnp.float32(scale)
    stop_band = damp * jnp.float32(scale)
    lane = lax.broadcasted_iota(jnp.int32, (rows, width), 1)
    back = []
    for k, (a, b) in enumerate(places):
        wave = k + segments * lane
        response = jnp.where(jnp.minimum(wave, total - wave) <= cut, pass_band, stop_band)
        re, im = pick(product, a, 0), -pick(product, a, 1)
        if b is not None:
            re, im = re + pick(product, b, 1), im + pick(product, b, 0)
        back.append((put(re * response), put(im * response)))
    product = multiply()
    spectrum = []
    for k, (a, b) in enumerate(back):
        re = pick(product, a, 0) - pick(product, b, 1)
        if k == 0:
            spectrum.append((re, None))
            continue
        im = pick(product, b, 0) + pick(product, a, 1)
        c, s = twiddle[2 * k : 2 * k + 1, :], twiddle[2 * k + 1 : 2 * k + 2, :]
        if k == half:
            spectrum.append((re * c - im * s, None))
        else:
            spectrum.append((re * c - im * s, im * c + re * s))
    return real_idft(spectrum)


def spans(start, count, rows_dev, channels):
    pieces, at, end = [], start, min(start + count, channels * rows_dev)
    while at < end:
        channel, row = divmod(at, rows_dev)
        take = min(end - at, rows_dev - row)
        pieces.append((at - start, channel, row, take))
        at += take
    return pieces


def partners(me, count):
    bits = count.bit_length() - 1
    half = count // 2
    order = [p for q in range(half) for p in (half + (half - 1 - q), q) if p]
    flipped = []
    for p in order:
        other = 0
        for i in range(bits):
            bit = lax.rem(me // (1 << i), 2)
            other = other + (1 << i) * ((1 - bit) if (p >> i) & 1 else bit)
        flipped.append(other)
    return flipped


def pad_lanes(value, width):
    rows, length = value.shape
    if width == length:
        return value
    return jnp.concatenate([value, jnp.zeros((rows, width - length), value.dtype)], axis=1)


def step_kernel(
    segments, bands, chunks, share,
    fields_hbm, east_hbm, north_hbm, cutoff, damping, ship, weight_hbm, twiddle, out_ref, kept_hbm, polar,
    cells, kept, east, north, weight, facts, edge_out, edge_in, advected, gathered, results,
    returned, spread, cut_ref, damp_ref,
    load_sem, halo_send, halo_recv, send_a, recv_a, send_b, recv_b,
):
    channels, rows_dev, length = fields_hbm.shape
    width = advected.shape[2]
    lat_count = rows_dev * bands
    body = pl.ds(8, rows_dev)
    me, band = lax.axis_index("lon"), lax.axis_index("lat")
    right, left = lax.rem(me + 1, segments), lax.rem(me + segments - 1, segments)
    peers = partners(me, segments)
    loads = [
        pltpu.make_async_copy(fields_hbm, cells.at[:, body], load_sem.at[0]),
        pltpu.make_async_copy(north_hbm, north.at[body], load_sem.at[1]),
        pltpu.make_async_copy(east_hbm, east, load_sem.at[2]),
        pltpu.make_async_copy(weight_hbm, weight, load_sem.at[3]),
    ]
    for load in loads:
        load.start()
    barrier = pltpu.get_barrier_semaphore()
    for peer in peers:
        pl.semaphore_signal(barrier, inc=1, device_id={"lon": peer}, device_id_type=MESH)

    @pl.when(band > 0)
    def _():
        pl.semaphore_signal(barrier, inc=1, device_id={"lat": band - 1}, device_id_type=MESH)

    @pl.when(band < bands - 1)
    def _():
        pl.semaphore_signal(barrier, inc=1, device_id={"lat": band + 1}, device_id_type=MESH)

    @pl.when(band == 0)
    def _():
        cells[:, 0:8, :] = jnp.zeros((channels, 8, length), jnp.float32)
        north[0:8, :] = jnp.zeros((8, length), jnp.float32)

    @pl.when(band == bands - 1)
    def _():
        cells[:, rows_dev + 8 : rows_dev + 16, :] = jnp.zeros((channels, 8, length), jnp.float32)

    row = band * rows_dev + lax.broadcasted_iota(jnp.int32, (rows_dev, 128), 0)
    lane = lax.broadcasted_iota(jnp.int32, (rows_dev, 128), 1)
    shift = jnp.where(lane == 0, 1.0, jnp.where(lane == 1, 0.0, 0.5))
    facts[...] = jnp.sin((row.astype(jnp.float32) + shift) * (math.pi / lat_count))

    for load in loads[:3]:
        load.wait()
    for c in range(channels):
        edge_out[0, :, c : c + 1] = cells[c, body, length - 1 : length]
        edge_out[1, :, c : c + 1] = cells[c, body, 0:1]
    edge_out[0, :, channels : channels + 1] = east[:, length - 1 : length]
    beside = jnp.where(band > 0, 1, 0) + jnp.where(band < bands - 1, 1, 0)
    pl.semaphore_wait(barrier, segments - 1 + beside)

    def halo(source, target, slot, place):
        return pltpu.make_async_remote_copy(
            src_ref=source, dst_ref=target, send_sem=halo_send.at[slot],
            recv_sem=halo_recv.at[slot], device_id=place, device_id_type=MESH,
        )

    first, last = pl.ds(8, 8), pl.ds(rows_dev, 8)
    above = pl.ds(rows_dev + 8, 8)
    up = {"lat": jnp.minimum(band + 1, bands - 1)}
    down = {"lat": jnp.maximum(band - 1, 0)}
    northward = [
        halo(cells.at[:, last], cells.at[:, pl.ds(0, 8)], 0, up),
        halo(north.at[last], north.at[pl.ds(0, 8)], 1, up),
    ]
    southward = halo(cells.at[:, first], cells.at[:, above], 2, down)
    sideways = [
        halo(edge_out.at[0], edge_in.at[0], 3, {"lon": right}),
        halo(edge_out.at[1], edge_in.at[1], 4, {"lon": left}),
    ]
    for copy in sideways:
        copy.start()

    @pl.when(band < bands - 1)
    def _():
        for copy in northward:
            copy.start()

    @pl.when(band > 0)
    def _():
        southward.start()

    flat = me * share + lax.broadcasted_iota(jnp.int32, (share, lat_count), 0)
    wanted = band * rows_dev + lax.rem(flat, rows_dev)
    hit = wanted == lax.broadcasted_iota(jnp.int32, (share, lat_count), 1)
    cut_ref[...] = jnp.sum(jnp.where(hit, cutoff[...].astype(jnp.float32), 0.0), axis=1, keepdims=True)
    damp_ref[...] = jnp.sum(jnp.where(hit, damping[...], 0.0), axis=1, keepdims=True)
    own = lax.broadcasted_iota(jnp.int32, (rows_dev, ship.shape[2]), 0)
    lists = ship[band]
    found = jnp.zeros(own.shape, jnp.float32)
    for d in range(bands):
        found += jnp.where(own == lists[d : d + 1, :], 1.0, 0.0)
    polar[...] = jnp.sum(found, axis=1, keepdims=True)
    spread[...] = jnp.zeros_like(spread)
    for j in range(segments):
        filled = min(max(channels * rows_dev - j * share, 0), share)
        if filled < share:
            advected[j, filled:share, :] = jnp.zeros((share - filled, width), jnp.float32)

    for copy in sideways:
        copy.wait()

    @pl.when(band < bands - 1)
    def _():
        for copy in northward:
            copy.wait_send()
        southward.wait_recv()

    @pl.when(band > 0)
    def _():
        southward.wait_send()
        for copy in northward:
            copy.wait_recv()

    def advect(channel, r, rows):
        here = pl.ds(r, rows)
        field = pad_lanes(cells[channel, pl.ds(r + 8, rows), :], width)
        upper = pad_lanes(cells[channel, pl.ds(r + 9, rows), :], width)
        lower = pad_lanes(cells[channel, pl.ds(r + 7, rows), :], width)
        courant_e = pad_lanes(east[here, :], width)
        courant_n = pad_lanes(north[pl.ds(r + 8, rows), :], width)
        courant_s = pad_lanes(north[pl.ds(r + 7, rows), :], width)
        column = lax.broadcasted_iota(jnp.int32, (rows, width), 1)
        grow = band * rows_dev + r + lax.broadcasted_iota(jnp.int32, (rows, 1), 0)
        east_cell = edge_in[1, here, channel : channel + 1]
        west_cell = edge_in[0, here, channel : channel + 1]
        west_courant = edge_in[0, here, channels : channels + 1]
        ahead = jnp.where(column == length - 1, east_cell, pltpu.roll(field, width - 1, 1))
        east_flux = courant_e * jnp.where(courant_e > 0, field, ahead)
        entering = west_courant * jnp.where(west_courant > 0, west_cell, field[:, 0:1])
        west_flux = jnp.where(column == 0, entering, pltpu.roll(east_flux, 1, 1))
        west_flux = jnp.where(column < length, west_flux, 0.0)
        face_n, face_s = facts[here, 0:1], facts[here, 1:2]
        north_flux = courant_n * jnp.where(courant_n > 0, field, upper) * face_n
        south_flux = courant_s * jnp.where(courant_s > 0, lower, field) * face_s
        north_flux = jnp.where(grow < lat_count - 1, north_flux, 0.0)
        south_flux = jnp.where(grow > 0, south_flux, 0.0)
        return field - (east_flux - west_flux) - (north_flux - south_flux) * (1.0 / facts[here, 2:3])

    outward, homeward = [], []
    for c, (start, rows) in enumerate(chunks):
        window = pl.ds(start, rows)
        for j in range(segments):
            for offset, channel, r, count in spans(j * share + start, rows, rows_dev, channels):
                value = advect(channel, r, count)
                advected[j, start + offset : start + offset + count, :] = value
                kept[channel, r : r + count, :] = value[:, :length]
        for p, peer in enumerate(peers):
            copy = pltpu.make_async_remote_copy(
                src_ref=advected.at[peer, window],
                dst_ref=gathered.at[me, window],
                send_sem=send_a.at[c, p],
                recv_sem=recv_a.at[c, p],
                device_id={"lon": peer},
                device_id_type=MESH,
            )
            copy.start()
            outward.append(copy)
    keep = pltpu.make_async_copy(kept, kept_hbm, load_sem.at[4])
    keep.start()
    loads[3].wait()
    for c, (start, rows) in enumerate(chunks):
        window = pl.ds(start, rows)
        gathered[me, window] = advected[me, window]
        for p in range(segments - 1):
            outward[c * (segments - 1) + p].wait_recv()
        filtered = filter_rows(
            [gathered[j, window] for j in range(segments)],
            cut_ref[window, :].astype(jnp.int32), damp_ref[window, :], weight, twiddle, spread,
            length,
        )
        for j in range(segments):
            results[j, window] = filtered[j]
        for p, peer in enumerate(peers):
            copy = pltpu.make_async_remote_copy(
                src_ref=results.at[peer, window],
                dst_ref=returned.at[me, window],
                send_sem=send_b.at[c, p],
                recv_sem=recv_b.at[c, p],
                device_id={"lon": peer},
                device_id_type=MESH,
            )
            copy.start()
            homeward.append(copy)
        returned[me, window] = results[me, window]
    for c, (start, rows) in enumerate(chunks):
        for p in range(segments - 1):
            homeward[c * (segments - 1) + p].wait_recv()
        for j in range(segments):
            for offset, channel, r, count in spans(j * share + start, rows, rows_dev, channels):
                here = slice(start + offset, start + offset + count)
                out_ref[channel, r : r + count, :] = returned[j, here, :][:, :length]
    for copy in outward + homeward:
        copy.wait_send()
    keep.wait()


def per_device(pieces, fields, east_courant, north_courant, cutoff, damping, ship_rows):
    channels, rows_dev, length = fields.shape
    segments, bands = lax.axis_size("lon"), lax.axis_size("lat")
    width = ceil_to(length, 128)
    share = ceil_to(ceil_to(channels * rows_dev, segments) // segments, 8)
    chunks = chunk_rows(share, pieces)
    weight, twiddle = tables(segments, length, width)
    depth = (segments + 2) * ceil_to(max(rows for _, rows in chunks), 16)
    semaphores = pltpu.SemaphoreType.DMA((len(chunks), segments - 1))
    block = pltpu.VMEM((segments, share, width), jnp.float32)
    whole, local = pl.BlockSpec(memory_space=pl.ANY), pl.BlockSpec(memory_space=pltpu.VMEM)
    filtered, advected, polar = pl.pallas_call(
        functools.partial(step_kernel, segments, bands, chunks, share),
        out_shape=[
            jax.ShapeDtypeStruct(fields.shape, jnp.float32),
            jax.ShapeDtypeStruct(fields.shape, jnp.float32),
            jax.ShapeDtypeStruct((rows_dev, 1), jnp.float32),
        ],
        in_specs=[whole, whole, whole, local, local, local, whole, local],
        out_specs=[local, whole, local],
        scratch_shapes=[
            pltpu.VMEM((channels, rows_dev + 16, length), jnp.float32),
            pltpu.VMEM(fields.shape, jnp.float32),
            pltpu.VMEM((rows_dev, length), jnp.float32),
            pltpu.VMEM((rows_dev + 16, length), jnp.float32),
            pltpu.VMEM(weight.shape, BF16),
            pltpu.VMEM((rows_dev, 128), jnp.float32),
            pltpu.VMEM((2, rows_dev, 128), jnp.float32),
            pltpu.VMEM((2, rows_dev, 128), jnp.float32),
            block, block, block, block,
            pltpu.VMEM((depth, 3 * width), BF16),
            pltpu.VMEM((share, 1), jnp.float32),
            pltpu.VMEM((share, 1), jnp.float32),
            pltpu.SemaphoreType.DMA((5,)),
            pltpu.SemaphoreType.DMA((5,)),
            pltpu.SemaphoreType.DMA((5,)),
            semaphores, semaphores, semaphores, semaphores,
        ],
        compiler_params=pltpu.CompilerParams(
            collective_id=0, has_side_effects=True, vmem_limit_bytes=56 * 1024 * 1024
        ),
    )(
        fields, east_courant, north_courant, cutoff[None, :], damping[None, :],
        ship_rows, jnp.asarray(weight), jnp.asarray(twiddle),
    )
    return jnp.where(polar[None] > 0.0, filtered, advected)


def solution(mesh):
    placed = (P(None, "lat", "lon"), P("lat", "lon"), P("lat", "lon"), P(), P(), P())
    return jax.shard_map(
        functools.partial(per_device, 5), mesh=mesh, in_specs=placed, out_specs=P(None, "lat", "lon"), check_vma=False
    )
```
